1024 devices in a mesh: batch: 64 (over y, z), proto: 16 (over x, core).
Axes of the slice: x: 8, y: 8, z: 8, core: 2. Of those that a mesh axis runs over, the one named last changes fastest.
Arguments:
- features: bfloat16 [8192, 1536], P('batch'), may hold values from -20 to 20
- w_first: bfloat16 [1536, 4096], P(None, 'proto'), may hold values from -0.15625 to 0.15625
- bn_gain: float32 [4096], P('proto'), may hold values from 0.1 to 1.9
- bn_shift: float32 [4096], P('proto'), may hold values from -3 to 3
- w_second: bfloat16 [4096, 256], P('proto'), may hold values from -1 to 1
- prototypes: bfloat16 [65536, 256], P('proto'), may hold values from -6 to 6
- partner: int32 [8192], P('batch'), may hold values from 0 to 127, as said below
Outputs:
- crop_penalty: float32 [8192], P('batch')
- grad_w1: float32 [1536, 4096], P('batch', 'proto')
- grad_gain: float32 [4096], P('proto')
- grad_shift: float32 [4096], P('proto')
- grad_w2: float32 [4096, 256], P('proto', 'batch')
The draws below stay inside these ranges and needn't reach their ends.
Inputs may be any that keep to these rules, and one draw needn't show every extreme that they name: partner_i is a crop index within crop i's group of 128 consecutive crops; the partner of partner_i is i, and partner_i is never i.
All inputs are finite; a program needn't handle non-finite values.
Results may differ from the reference program's by a relative error of at most 0.015.
Values sent between devices are 32-bit elements; how exact they have to be, the bound alone decides.
A program may use at most 32 MiB of HBM per device.

```python
import jax
import jax.numpy as jnp
from jax import lax

D_IN = 1536
HIDDEN_UNITS = 4096
EMB = 256
CROP_DEV = 128
ITERS = 3
PROTOS = 65536
CROPS = 8192


def draw_features(key, part):
    first_key = jax.random.fold_in(key, 0)
    row_ramp = 1.0 + 2.0 * jnp.arange(CROPS, dtype=jnp.float32)[:, None] / max(CROPS - 1, 1)
    values = jax.random.normal(first_key, (CROPS, D_IN), jnp.float32) * row_ramp
    return jnp.clip(values, -20.0, 20.0).astype(jnp.bfloat16)


def shared_signs(key):
    flips = jax.random.bernoulli(jax.random.fold_in(key, 7), 0.5, (EMB,))
    return 2.0 * flips.astype(jnp.float32) - 1.0


def draw_w_second(key, part):
    signs = shared_signs(key)
    noise_key, along_key = jax.random.split(jax.random.fold_in(key, 11))
    noise = jnp.clip(jax.random.normal(noise_key, (HIDDEN_UNITS, EMB), jnp.float32), -4.0, 4.0)
    along = jnp.clip(jax.random.normal(along_key, (HIDDEN_UNITS,), jnp.float32), -3.0, 3.0)
    values = (noise + along[:, None] * signs[None, :]) * HIDDEN_UNITS ** (-0.5)
    return values.astype(jnp.bfloat16)


def draw_prototypes(key, part):
    signs = shared_signs(key)
    noise_key, along_key = jax.random.split(jax.random.fold_in(key, 13), 2)
    noise = jnp.clip(jax.random.normal(noise_key, (PROTOS, EMB), jnp.float32), -4.0, 4.0)
    along = jax.random.uniform(along_key, (PROTOS,), jnp.float32, -1.5, 1.5)
    values = noise + along[:, None] * signs[None, :]
    return values.astype(jnp.bfloat16)


def shuffle(subkey):
    return jax.random.permutation(subkey, CROP_DEV)


def draw_partner(key, part):
    groups = CROPS // CROP_DEV
    orders = jax.vmap(shuffle)(jax.random.split(key, groups))
    swapped = orders.reshape(groups, CROP_DEV // 2, 2)[:, :, ::-1].reshape(groups, CROP_DEV)
    inverse = jnp.argsort(orders, axis=1)
    paired = jnp.take_along_axis(swapped, inverse, axis=1)
    return paired.reshape(CROPS).astype(jnp.int32)


def shard_levels(key, shape, pieces, least, high):
    loudness, own = 1.0, jax.random.fold_in(key, 6)
    for dim, shards_of in pieces:
        heights = jnp.exp(jax.random.uniform(jax.random.fold_in(own, dim), (shards_of,), jnp.float32, least / len(pieces), high / len(pieces)))
        loudness = loudness * jnp.repeat(heights, shape[dim] // shards_of).reshape([-1 if axis == dim else 1 for axis in range(len(shape))])
    return loudness


def centred(rng, dims, scale, most, cuts=(), kind=jnp.bfloat16):
    factor_of = shard_levels(rng, dims, cuts, -0.22, 0.18) if cuts else 1.0
    values = jax.random.normal(rng, dims, jnp.float32) * scale * factor_of
    return jnp.minimum(jnp.maximum(values, -most), most).astype(kind)


def setup_inputs(seed: int = 0) -> dict:
    key_of = jax.random.split(jax.random.key(seed), 8)
    features = draw_features(jax.random.fold_in(key_of[7], 71), 0)
    w_first = centred(key_of[1], (D_IN, HIDDEN_UNITS), D_IN ** -0.5, 0.15625, ((1, 16),))
    bn_gain = jnp.clip(1.0 + 0.18 * jax.random.normal(key_of[2], (HIDDEN_UNITS,), jnp.float32), 0.1, 1.9)
    bn_shift = centred(key_of[3], (HIDDEN_UNITS,), 0.5, 3.0, ((0, 16),), jnp.float32)
    w_second = draw_w_second(jax.random.fold_in(key_of[7], 71), 0)
    prototypes = draw_prototypes(jax.random.fold_in(key_of[7], 71), 0)
    partner = draw_partner(jax.random.fold_in(key_of[7], 71), 0)
    return {"features": features, "w_first": w_first, "bn_gain": bn_gain, "bn_shift": bn_shift, "w_second": w_second, "prototypes": prototypes, "partner": partner}


balancing_epsilon = 0.05
sharpness_divisor = 0.1
penalty_weighting = 64.0

def reference(features, w_first, bn_gain, bn_shift, w_second, prototypes, partner):
    f32 = jnp.float32
    pre_act = jnp.dot(features, w_first, preferred_element_type=f32)
    batch_mean = lax.optimization_barrier(jnp.sum(pre_act, 0)) / CROPS
    batch_var = lax.optimization_barrier(jnp.sum(pre_act * pre_act, 0)) / CROPS - batch_mean * batch_mean
    inv_std = lax.rsqrt(batch_var + 1e-05)
    normed = (pre_act - batch_mean) * inv_std
    shifted = bn_gain * normed + bn_shift
    hidden = jnp.maximum(shifted, 0.0).astype(jnp.bfloat16)
    raw_emb = jnp.dot(hidden, w_second, preferred_element_type=f32)
    inv_norm = lax.rsqrt(lax.optimization_barrier(jnp.sum(raw_emb * raw_emb, 1, keepdims=True)) + 1e-06)
    embedded = raw_emb * inv_norm
    emb_low = embedded.astype(jnp.bfloat16)
    proto_float = prototypes.astype(f32)
    unit_protos = (proto_float * lax.rsqrt(lax.optimization_barrier(jnp.sum(proto_float * proto_float, 1, keepdims=True)) + 1e-06)).astype(jnp.bfloat16)
    groups = CROPS // CROP_DEV
    emb_blocks = emb_low.reshape(groups, CROP_DEV, EMB)
    partner_blocks = partner.reshape(groups, CROP_DEV)

    def scores_in_block(block_slice):
        return lax.dot_general(block_slice, unit_protos, (((1,), (1,)), ((), ())), preferred_element_type=f32)

    def first_step(running, block_slice):
        exponent_codes = jnp.exp(scores_in_block(block_slice) / balancing_epsilon)
        ones_rows = jnp.ones((CROP_DEV,), f32)
        return (running + jnp.dot(ones_rows, exponent_codes, precision=lax.Precision.HIGHEST), None)
    col_mass, unused = lax.scan(first_step, jnp.zeros((PROTOS,), f32), emb_blocks)
    scale_cols = 1.0 / col_mass

    def make_step(current_cols):

        def later_step(running, block_slice):
            exponent_codes = jnp.exp(scores_in_block(block_slice) / balancing_epsilon)
            rows = 1.0 / lax.optimization_barrier(jnp.sum(exponent_codes * current_cols, 1))
            return (running + jnp.dot(rows, exponent_codes, precision=lax.Precision.HIGHEST), None)
        return later_step
    for iteration in range(ITERS - 1):
        col_mass, unused = lax.scan(make_step(scale_cols), jnp.zeros((PROTOS,), f32), emb_blocks)
        scale_cols = 1.0 / col_mass

    def final_pass(pair):
        block_slice, partners = pair
        centroid_affinity = scores_in_block(block_slice)
        exponent_codes = jnp.exp(centroid_affinity / balancing_epsilon)
        weighted = exponent_codes * scale_cols
        rows = 1.0 / lax.optimization_barrier(jnp.sum(weighted, 1))
        codes = weighted * rows[:, None]
        desired_assignments = jnp.take(codes, partners, axis=0)
        raised_affinity = jnp.exp(centroid_affinity / sharpness_divisor)
        partition_total = lax.optimization_barrier(jnp.sum(raised_affinity, 1))
        penalty_array = jnp.log(partition_total) - lax.optimization_barrier(jnp.sum(desired_assignments * centroid_affinity, 1)) / sharpness_divisor
        normalized_likelihood = raised_affinity / partition_total[:, None]
        affinity_derivative = (penalty_weighting * (normalized_likelihood - desired_assignments) / sharpness_divisor).astype(jnp.bfloat16)
        emb_grad = jnp.dot(affinity_derivative, unit_protos, preferred_element_type=f32)
        return (penalty_array, emb_grad)
    loss_blocks, grad_blocks = lax.map(final_pass, (emb_blocks, partner_blocks))
    crop_penalty = loss_blocks.reshape(CROPS)
    emb_grad = grad_blocks.reshape(CROPS, EMB)
    inner_prod = lax.optimization_barrier(jnp.sum(embedded * emb_grad, 1, keepdims=True))
    raw_grad = ((emb_grad - embedded * inner_prod) * inv_norm).astype(jnp.bfloat16)
    grad_w2 = lax.dot_general(hidden, raw_grad, (((0,), (0,)), ((), ())), preferred_element_type=f32)
    hidden_grad = lax.dot_general(raw_grad, w_second, (((1,), (1,)), ((), ())), preferred_element_type=f32)
    bn_grad = jnp.where(shifted > 0, hidden_grad, 0.0)
    grad_shift = lax.optimization_barrier(jnp.sum(bn_grad, 0))
    grad_gain = lax.optimization_barrier(jnp.sum(bn_grad * normed, 0))
    pre_grad = (bn_gain * inv_std * (bn_grad - grad_shift / CROPS - normed * grad_gain / CROPS)).astype(jnp.bfloat16)
    grad_w1 = lax.dot_general(features, pre_grad, (((0,), (0,)), ((), ())), preferred_element_type=f32)
    return (crop_penalty, grad_w1, grad_gain, grad_shift, grad_w2)
```

```python
from types import SimpleNamespace

import jax
import jax.numpy as jnp
from jax import lax
from jax.experimental import pallas as pl
from jax.experimental.pallas import tpu as pltpu
from jax.sharding import PartitionSpec as P

ITERS = 3
MESH = pl.DeviceIdType.MESH
f32, bf16 = jnp.float32, jnp.bfloat16
CONTRACT_LAST = (((1,), (1,)), ((), ()))
CONTRACT_FIRST = (((0,), (0,)), ((), ()))

penalty_weighting = 64.0


def total(ref):
    count = ref.shape[0]
    chains = 4 if count >= 16 else 1
    sums = [ref[chain] for chain in range(chains)]
    for slot in range(chains, count):
        sums[slot % chains] = sums[slot % chains] + ref[slot]
    while len(sums) > 1:
        sums = [sums[i] + sums[i + 1] for i in range(0, len(sums), 2)]
    return sums[0]


def split(value):
    high = value.astype(bf16)
    low = (value - high.astype(f32)).astype(bf16)
    return jnp.concatenate([high, low], 0)


def make_kernel(ny, nz, npr, names, crops_all):
    def kernel(*refs):
        r = SimpleNamespace(**dict(zip(names, refs)))
        batch, proto = lax.axis_index("batch"), lax.axis_index("proto")
        y, z = batch // nz, batch % nz
        rings = {
            "y": (ny, y, lambda q: (q * nz + z, proto)),
            "z": (nz, z, lambda q: (y * nz + q, proto)),
            "p": (npr, proto, lambda q: (batch, q)),
        }
        send_sem, recv_sem, in_sem = r.send_sem, r.recv_sem, r.in_sem
        stages = []

        def send(source, target, stage, device):
            pltpu.make_async_remote_copy(
                src_ref=source,
                dst_ref=target,
                send_sem=send_sem.at[stage],
                recv_sem=recv_sem.at[stage],
                device_id=device,
                device_id_type=MESH,
            ).start()

        def new_stage(part):
            stages.append(part)
            return len(stages) - 1

        def exchange(axis, source_of, landing):
            count, me, device = rings[axis]
            stage = new_stage(landing.at[pl.ds(0, count - 1)])

            def step(offset, carry):
                peer = (me + offset) % count
                send(source_of(peer), landing.at[me], stage, device(peer))
                return carry

            lax.fori_loop(1, count, step, 0)
            landing[me] = source_of(me)[...]
            return stage

        def arrived(stage):
            pltpu.make_async_copy(stages[stage], stages[stage], recv_sem.at[stage]).wait()

        def sent(stage):
            pltpu.make_async_copy(stages[stage], stages[stage], send_sem.at[stage]).wait()

        def scatter(axis, source, landing, relay):
            count, me, device = rings[axis]
            far = count // 2
            stage_r, stage = new_stage(relay), new_stage(landing)
            back = (me + count - 1) % count
            send(source.at[(me + far) % count], relay, stage_r, device(back))
            near = [o for d in range(far - 1, 0, -1) for o in (d, count - d) if o != far + 1]
            for slot, offset in enumerate(near):
                peer = (me + offset) % count
                send(source.at[peer], landing.at[slot], stage, device(peer))

            def pass_on():
                arrived(stage_r)
                peer = (me + far + 1) % count
                source[peer] = source[peer] + relay[...]
                send(source.at[peer], landing.at[len(near)], stage, device(peer))

            def result():
                arrived(stage)
                return total(landing) + source[me]

            return pass_on, result

        loads = [
            pltpu.make_async_copy(src, dst, in_sem.at[i])
            for i, (src, dst) in enumerate(
                (
                    (r.f_in, r.f),
                    (r.w1_in, r.w1),
                    (r.w2_in, r.w2),
                    (r.pr_in, r.pr),
                    (r.gain_in, r.gain),
                    (r.shift_in, r.shift),
                    (r.partner_in, r.partner),
                )
            )
        ]
        for load in loads:
            load.start()

        barrier = pltpu.get_barrier_semaphore()
        peers = 0
        for axis in ("y", "z", "p"):
            count, me, device = rings[axis]
            peers += count - 1

            def greet(offset, carry, count=count, me=me, device=device):
                pl.semaphore_signal(
                    barrier, inc=1, device_id=device((me + offset) % count), device_id_type=MESH
                )
                return carry

            lax.fori_loop(1, count, greet, 0)

        loads[0].wait()
        loads[1].wait()
        pre_act = jnp.dot(r.f[...], r.w1[...], preferred_element_type=f32)
        r.pre[...] = pre_act
        r.mom[0:1, :] = jnp.sum(pre_act, 0, keepdims=True)
        r.mom[1:2, :] = jnp.sum(pre_act * pre_act, 0, keepdims=True)
        pl.semaphore_wait(barrier, peers)
        stage = exchange("y", lambda q: r.mom, r.mom_y)
        r.fsum[...] = jnp.sum(r.f[...].astype(f32), 0, keepdims=True)
        stage_f = exchange("y", lambda q: r.fsum, r.fsum_y)
        rows, emb = r.f.shape[0], r.w2.shape[1]
        lanes = 128
        slab, piece = r.ft.shape[1], r.grad_w1.shape[0]
        features_t = r.f[...].astype(f32).T.astype(bf16).reshape(ny, slab, rows)
        r.ft[:, :, :rows] = features_t
        r.ft[:, :, rows:] = features_t
        arrived(stage)
        r.mom2[...] = total(r.mom_y)
        stage = exchange("z", lambda q: r.mom2, r.mom_z)

        def by_features(right, left_out, right_out):
            def step(i, carry):
                grad = jnp.dot(r.ft[i], right[...], preferred_element_type=f32)
                left_out[i] = grad[:, :lanes].reshape(nz, piece, lanes)
                for q in range(nz):
                    right_out[q, i] = grad[q * piece : (q + 1) * piece, lanes:]
                return carry

            lax.fori_loop(0, ny, step, 0)

        r.pair[0] = split(r.pre[...])
        by_features(r.pair.at[0], r.fna, r.fnb)
        pass_a, early_a = scatter("y", r.fna, r.fna_y, r.fna_r)
        pass_b, early_b = scatter("z", r.fnb, r.fnb_z, r.fnb_r)
        for load in loads[2:]:
            load.wait()
        arrived(stage)
        moments = total(r.mom_z)
        batch_mean = moments[0:1, :] / crops_all
        batch_var = moments[1:2, :] / crops_all - batch_mean * batch_mean
        inv_std = lax.rsqrt(batch_var + 1e-05)
        gain, shift = r.gain[...], r.shift[...]
        normed = (r.pre[...] - batch_mean) * inv_std
        shifted = gain * normed + shift
        hidden = jnp.maximum(shifted, 0.0).astype(bf16)
        r.normed[...] = normed
        r.shifted[...] = shifted
        r.hidden[...] = hidden

        part = jnp.dot(hidden, r.w2[...], preferred_element_type=f32)
        r.emb_part[...] = part.reshape(r.emb_part.shape)
        stage = exchange("p", lambda q: r.emb_part.at[q], r.emb_rs)

        chunks, width = r.u.shape[0], r.u.shape[1]

        def unit(j, carry):
            proto_float = r.pr[j].astype(f32)
            inv = lax.rsqrt(jnp.sum(proto_float * proto_float, 1, keepdims=True) + 1e-06)
            r.u[j] = (proto_float * inv).astype(bf16)
            return carry

        lax.fori_loop(0, chunks // 2, unit, 0)
        pass_a()
        pass_b()
        arrived(stage)
        r.emb_own[...] = total(r.emb_rs)
        stage = exchange("p", lambda q: r.emb_own, r.emb_ag)
        lax.fori_loop(chunks // 2, chunks, unit, 0)
        arrived(stage_f)
        r.fsum2[...] = total(r.fsum_y)
        stage_f = exchange("z", lambda q: r.fsum2, r.fsum_z)
        arrived(stage)
        raw_emb = r.emb_ag[...].reshape(rows, emb)
        inv_norm = lax.rsqrt(jnp.sum(raw_emb * raw_emb, 1, keepdims=True) + 1e-06)
        embedded = raw_emb * inv_norm
        emb_low = embedded.astype(bf16)
        r.embedded[...] = embedded
        r.emb_low[...] = emb_low
        r.inv_norm[...] = jnp.broadcast_to(inv_norm, r.inv_norm.shape)

        half = width // 2
        groups = width // lanes

        def columns(j, codes):
            mass = jnp.sum(codes, 0, keepdims=True)
            r.col_a[0, pl.ds(j, 1), :] = mass[:, :half]
            r.col_b[0, pl.ds(j, 1), :] = mass[:, half:]

        def score(j, acc):
            affinity = lax.dot_general(
                r.emb_low[...], r.u[j], CONTRACT_LAST, preferred_element_type=f32
            )
            raised = jnp.exp(affinity * 10.0)
            codes = raised * raised
            r.codes[j] = codes
            r.raised[j] = raised.astype(bf16)
            columns(j, codes)
            for g in range(groups):
                acc = acc + raised[:, g * lanes : (g + 1) * lanes]
            return acc

        denom_part = lax.fori_loop(0, chunks, score, jnp.zeros((rows, lanes), f32))

        def to_row(square):
            return jnp.sum(square.T, 0, keepdims=True)

        def to_columns(row):
            return jnp.broadcast_to(row, (rows, lanes)).T

        def row_sums(scale):
            def step(j, acc):
                codes = r.codes[j]
                weight_a = codes[:, :half] * r.scale_a[pl.ds(j, 1), :]
                weight_b = codes[:, half:] * r.scale_b[pl.ds(j, 1), :]
                for g in range(half // lanes):
                    acc = acc + weight_a[:, g * lanes : (g + 1) * lanes]
                    acc = acc + weight_b[:, g * lanes : (g + 1) * lanes]
                return acc

            return to_row(lax.fori_loop(0, chunks, step, jnp.zeros((rows, lanes), f32)))

        for it in range(ITERS):
            stage_a = exchange("y", lambda q: r.col_a.at[it], r.col_a1.at[it])
            stage_b = exchange("z", lambda q: r.col_b.at[it], r.col_b1.at[it])
            if it == 0:
                def soft(j, acc):
                    return acc + jnp.dot(r.raised[j], r.u[j], preferred_element_type=f32)

                soft_part = lax.fori_loop(0, chunks, soft, jnp.zeros((rows, emb), f32))
                r.soft_part[...] = soft_part.reshape(r.soft_part.shape)
                soft_rs = exchange("p", lambda q: r.soft_part.at[q], r.soft_rs)
                r.row_src[0, 1:2, :] = to_row(denom_part)
            if it == 1:
                arrived(soft_rs)
                r.soft_own[...] = total(r.soft_rs)
                soft_ag = exchange("p", lambda q: r.soft_own, r.soft_ag)
                r.row_src[1, 1:2, :] = jnp.zeros((1, lanes), f32)
                arrived(stage_f)
                wanted = batch * piece + lax.broadcasted_iota(jnp.int32, (piece, ny * slab), 0)
                here = lax.broadcasted_iota(jnp.int32, (piece, ny * slab), 1) == wanted
                r.fsum_own[...] = jnp.broadcast_to(
                    jnp.sum(jnp.where(here, total(r.fsum_z), 0.0), 1, keepdims=True), (piece, lanes)
                )
                r.fnas[...] = early_a()
                stage_na = exchange("z", lambda q: r.fnas.at[q], r.fna_z)
                r.fnbs[...] = early_b()
                stage_nb = exchange("y", lambda q: r.fnbs.at[q], r.fnb_y)
            if it == 2:
                arrived(stage_na)
                r.fn_own[:, :lanes] = total(r.fna_z)
                arrived(stage_nb)
                r.fn_own[:, lanes:] = total(r.fnb_y)
            arrived(stage_a)
            r.col_as[it] = total(r.col_a1.at[it])
            stage_a = exchange("z", lambda q: r.col_as.at[it], r.col_a2.at[it])
            arrived(stage_b)
            r.col_bs[it] = total(r.col_b1.at[it])
            stage_b = exchange("y", lambda q: r.col_bs.at[it], r.col_b2.at[it])
            arrived(stage_a)
            r.scale_a[...] = 1.0 / total(r.col_a2.at[it])
            arrived(stage_b)
            r.scale_b[...] = 1.0 / total(r.col_b2.at[it])
            if it == ITERS - 1:
                break
            r.row_src[it, 0:1, :] = row_sums(None)
            stage = exchange("p", lambda q: r.row_src.at[it], r.row_ag.at[it])
            arrived(stage)
            masses = total(r.row_ag.at[it])
            if it == 0:
                r.denom[...] = masses[1:2, :]
            r.scale_rows[...] = to_columns(1.0 / masses[0:1, :])

            def column_sums(j, carry):
                scale = r.scale_rows[...]
                masses = [
                    jnp.sum(r.codes[j, :, g * lanes : (g + 1) * lanes] * scale, 0, keepdims=True)
                    for g in range(groups)
                ]
                r.col_a[it + 1, pl.ds(j, 1), :] = jnp.concatenate(masses[: groups // 2], 1)
                r.col_b[it + 1, pl.ds(j, 1), :] = jnp.concatenate(masses[groups // 2 :], 1)
                return carry

            lax.fori_loop(0, chunks, column_sums, 0)

        def target(j, carry):
            acc, grad = carry
            codes = r.codes[j]
            weight_a = codes[:, :half] * r.scale_a[pl.ds(j, 1), :]
            weight_b = codes[:, half:] * r.scale_b[pl.ds(j, 1), :]
            for g in range(half // lanes):
                acc = acc + weight_a[:, g * lanes : (g + 1) * lanes]
                acc = acc + weight_b[:, g * lanes : (g + 1) * lanes]
            grad = grad + jnp.dot(
                weight_a.astype(bf16), r.u[j, :half], preferred_element_type=f32
            )
            grad = grad + jnp.dot(
                weight_b.astype(bf16), r.u[j, half:], preferred_element_type=f32
            )
            return acc, grad

        row_part, target_part = lax.fori_loop(
            0, chunks, target, (jnp.zeros((rows, lanes), f32), jnp.zeros((rows, emb), f32))
        )
        r.tgt_part[...] = target_part.reshape(r.tgt_part.shape)
        stage = exchange("p", lambda q: r.tgt_part.at[q], r.tgt_rs)
        r.row_last[...] = to_row(row_part)
        stage_r = exchange("p", lambda q: r.row_last, r.row_last_ag)
        arrived(stage)
        r.tgt_own[...] = total(r.tgt_rs)
        stage = exchange("p", lambda q: r.tgt_own, r.tgt_ag)
        arrived(soft_ag)
        arrived(stage_r)
        scale_last = to_columns(1.0 / total(r.row_last_ag))
        denom = r.denom[...]
        denom_columns = to_columns(1.0 / denom)
        rows_iota = lax.broadcasted_iota(jnp.int32, (rows, rows), 0)
        swap = jnp.where(r.partner[...] == rows_iota, 1.0, 0.0).astype(f32)
        wide = lambda x: jnp.concatenate([x, x], 1)
        soft_grad = r.soft_ag[...].reshape(rows, emb) * wide(denom_columns)
        arrived(stage)
        own_target = r.tgt_ag[...].reshape(rows, emb) * wide(scale_last)
        partner_target = jnp.dot(
            swap, own_target, precision=lax.Precision.HIGHEST, preferred_element_type=f32
        )
        emb_grad = (soft_grad - partner_target) * (penalty_weighting * 10.0)
        embedded = r.embedded[...]
        inner = jnp.sum(embedded * emb_grad, 1, keepdims=True)
        raw_grad = ((emb_grad - embedded * inner) * r.inv_norm[:, 0:1]).astype(bf16)

        hidden_grad = lax.dot_general(
            raw_grad, r.w2[...], CONTRACT_LAST, preferred_element_type=f32
        )
        bn_grad = jnp.where(r.shifted[...] > 0, hidden_grad, 0.0)
        r.gsum[0:1, :] = jnp.sum(bn_grad, 0, keepdims=True)
        r.gsum[1:2, :] = jnp.sum(bn_grad * r.normed[...], 0, keepdims=True)
        stage = exchange("y", lambda q: r.gsum, r.gsum_y)
        r.pair[1] = split(bn_grad)
        by_features(r.pair.at[1], r.g1a, r.g1b)
        pass_a, late_a = scatter("y", r.g1a, r.g1a_y, r.g1a_r)
        pass_b, late_b = scatter("z", r.g1b, r.g1b_z, r.g1b_r)
        w2_grad = lax.dot_general(
            raw_grad, r.hidden[...], CONTRACT_FIRST, preferred_element_type=f32
        )
        r.g2a[...] = w2_grad[:, :lanes].reshape(ny, nz // 2, 8, lanes)
        right = w2_grad[:, lanes:].reshape(ny // 2, 2, nz // 2, 8, lanes)
        upper = lax.broadcasted_iota(jnp.int32, (nz // 2, 8, lanes), 1) < 4
        for i in range(ny // 2):
            one, two = right[i, 0], right[i, 1]
            r.g2b[:, 0, i] = jnp.where(upper, one, pltpu.roll(two, 4, 1))
            r.g2b[:, 1, i] = jnp.where(upper, pltpu.roll(one, 4, 1), two)
        stage_2a = exchange("y", lambda q: r.g2a.at[q], r.g2a_y)
        stage_2b = exchange("z", lambda q: r.g2b.at[q // 2, q % 2], r.g2b_z)
        score_dot = r.emb_low[...].astype(f32) * partner_target
        mismatch = to_row(score_dot[:, :lanes] + score_dot[:, lanes:])
        r.penalty[...] = jnp.log(denom) - mismatch * 10.0
        arrived(stage)
        r.gsum2[...] = total(r.gsum_y)
        stage = exchange("z", lambda q: r.gsum2, r.gsum_z)
        pass_a()
        pass_b()
        arrived(stage)
        sums = total(r.gsum_z)
        grad_shift, grad_gain = sums[0:1, :], sums[1:2, :]
        r.grad_shift[...] = grad_shift
        r.grad_gain[...] = grad_gain
        scale = gain * inv_std
        fsum = jnp.concatenate([r.fsum_own[...], r.fsum_own[...]], 1)
        by_normed = (r.fn_own[...] - fsum * batch_mean) * inv_std
        known = fsum * (grad_shift / crops_all) + by_normed * (grad_gain / crops_all)
        arrived(stage_2a)
        r.g2as[...] = total(r.g2a_y)
        stage_2a = exchange("z", lambda q: r.g2as.at[q // 2], r.g2a_z)
        arrived(stage_2b)
        r.g2bs[...] = total(r.g2b_z)
        stage_2b = exchange("y", lambda q: r.g2bs.at[q // 2], r.g2b_y)
        r.g1as[...] = late_a()
        stage_a = exchange("z", lambda q: r.g1as.at[q], r.g1a_z)
        r.g1bs[...] = late_b()
        stage_b = exchange("y", lambda q: r.g1bs.at[q], r.g1b_y)

        def own_half(tile, place):
            return jnp.where(place % 2 == 1, pltpu.roll(tile, 4, 0), tile)[0:4]

        arrived(stage_2a)
        r.grad_w2[:, :lanes] = own_half(total(r.g2a_z), z)
        arrived(stage_2b)
        r.grad_w2[:, lanes:] = own_half(total(r.g2b_y), y)
        arrived(stage_a)
        r.grad_w1[:, :lanes] = scale[:, :lanes] * (total(r.g1a_z) - known[:, :lanes])
        arrived(stage_b)
        r.grad_w1[:, lanes:] = scale[:, lanes:] * (total(r.g1b_y) - known[:, lanes:])
        for stage in range(len(stages)):
            sent(stage)

    return kernel


def hand_over(*refs):
    count = len(refs) // 2
    copies = [pltpu.make_async_copy(refs[i], refs[count + i], refs[-1].at[i]) for i in range(count)]
    for copy in copies:
        copy.start()
    for copy in copies:
        copy.wait()


def solution(mesh):
    nb, npr = mesh.shape["batch"], mesh.shape["proto"]
    ny = 1
    while (2 * ny) ** 2 <= nb:
        ny *= 2
    nz = nb // ny

    def body(features, w_first, bn_gain, bn_shift, w_second, prototypes, partner):
        rows, d_in = features.shape
        units, emb = w_second.shape
        protos = prototypes.shape[0]
        chunks = 8
        width = protos // chunks
        half = width // 2
        lanes = 128
        block = rows // npr
        slab, piece = d_in // ny, d_in // nb
        vmem = pltpu.VMEM
        scratch = dict(
            f=vmem((rows, d_in), bf16),
            w1=vmem((d_in, units), bf16),
            gain=vmem((1, units), f32),
            shift=vmem((1, units), f32),
            partner=vmem((1, rows), jnp.int32),
            w2=vmem((units, emb), bf16),
            pr=vmem((chunks, width, emb), bf16),
            u=vmem((chunks, width, emb), bf16),
            ft=vmem((ny, slab, 2 * rows), bf16),
            pair=vmem((2, 2 * rows, units), bf16),
            pre=vmem((rows, units), f32),
            mom=vmem((2, units), f32),
            mom_y=vmem((ny, 2, units), f32),
            mom2=vmem((2, units), f32),
            mom_z=vmem((nz, 2, units), f32),
            fsum=vmem((1, d_in), f32),
            fsum_y=vmem((ny, 1, d_in), f32),
            fsum2=vmem((1, d_in), f32),
            fsum_z=vmem((nz, 1, d_in), f32),
            fsum_own=vmem((piece, lanes), f32),
            fna=vmem((ny, nz, piece, lanes), f32),
            fnb=vmem((nz, ny, piece, lanes), f32),
            fna_y=vmem((ny - 2, nz, piece, lanes), f32),
            fnb_z=vmem((nz - 2, ny, piece, lanes), f32),
            fnas=vmem((nz, piece, lanes), f32),
            fnbs=vmem((ny, piece, lanes), f32),
            fna_z=vmem((nz, piece, lanes), f32),
            fnb_y=vmem((ny, piece, lanes), f32),
            fn_own=vmem((piece, units), f32),
            normed=vmem((rows, units), f32),
            shifted=vmem((rows, units), f32),
            hidden=vmem((rows, units), bf16),
            emb_part=vmem((npr, block, emb), f32),
            emb_rs=vmem((npr, block, emb), f32),
            emb_own=vmem((block, emb), f32),
            emb_ag=vmem((npr, block, emb), f32),
            embedded=vmem((rows, emb), f32),
            emb_low=vmem((rows, emb), bf16),
            inv_norm=vmem((rows, lanes), f32),
            codes=vmem((chunks, rows, width), f32),
            raised=vmem((chunks, rows, width), bf16),
            col_a=vmem((ITERS, chunks, half), f32),
            col_b=vmem((ITERS, chunks, half), f32),
            col_a1=vmem((ITERS, ny, chunks, half), f32),
            col_b1=vmem((ITERS, nz, chunks, half), f32),
            col_as=vmem((ITERS, chunks, half), f32),
            col_bs=vmem((ITERS, chunks, half), f32),
            col_a2=vmem((ITERS, nz, chunks, half), f32),
            col_b2=vmem((ITERS, ny, chunks, half), f32),
            scale_a=vmem((chunks, half), f32),
            scale_b=vmem((chunks, half), f32),
            soft_part=vmem((npr, block, emb), f32),
            soft_rs=vmem((npr, block, emb), f32),
            soft_own=vmem((block, emb), f32),
            soft_ag=vmem((npr, block, emb), f32),
            row_src=vmem((ITERS - 1, 2, rows), f32),
            row_ag=vmem((ITERS - 1, npr, 2, rows), f32),
            denom=vmem((1, rows), f32),
            scale_rows=vmem((rows, lanes), f32),
            tgt_part=vmem((npr, block, emb), f32),
            tgt_rs=vmem((npr, block, emb), f32),
            tgt_own=vmem((block, emb), f32),
            tgt_ag=vmem((npr, block, emb), f32),
            row_last=vmem((1, rows), f32),
            row_last_ag=vmem((npr, 1, rows), f32),
            gsum=vmem((2, units), f32),
            gsum_y=vmem((ny, 2, units), f32),
            gsum2=vmem((2, units), f32),
            gsum_z=vmem((nz, 2, units), f32),
            g2a=vmem((ny, nz // 2, 8, lanes), f32),
            g2b=vmem((nz // 2, 2, ny // 2, 8, lanes), f32),
            g2a_y=vmem((ny, nz // 2, 8, lanes), f32),
            g2b_z=vmem((nz, ny // 2, 8, lanes), f32),
            g2as=vmem((nz // 2, 8, lanes), f32),
            g2bs=vmem((ny // 2, 8, lanes), f32),
            g2a_z=vmem((nz, 8, lanes), f32),
            g2b_y=vmem((ny, 8, lanes), f32),
            g1a_r=vmem((nz, piece, lanes), f32),
            g1b_r=vmem((ny, piece, lanes), f32),
            fna_r=vmem((nz, piece, lanes), f32),
            fnb_r=vmem((ny, piece, lanes), f32),
            g1a=vmem((ny, nz, piece, lanes), f32),
            g1b=vmem((nz, ny, piece, lanes), f32),
            g1a_y=vmem((ny - 2, nz, piece, lanes), f32),
            g1b_z=vmem((nz - 2, ny, piece, lanes), f32),
            g1as=vmem((nz, piece, lanes), f32),
            g1bs=vmem((ny, piece, lanes), f32),
            g1a_z=vmem((nz, piece, lanes), f32),
            g1b_y=vmem((ny, piece, lanes), f32),
            send_sem=pltpu.SemaphoreType.DMA((64,)),
            recv_sem=pltpu.SemaphoreType.DMA((64,)),
            in_sem=pltpu.SemaphoreType.DMA((7,)),
        )
        whole = pl.BlockSpec(memory_space=pl.ANY)
        here = pl.BlockSpec(memory_space=pltpu.VMEM)
        inputs = dict(
            f_in=features,
            w1_in=w_first,
            gain_in=bn_gain.reshape(1, units),
            shift_in=bn_shift.reshape(1, units),
            w2_in=w_second,
            pr_in=prototypes.reshape(chunks, width, emb),
            partner_in=partner.reshape(1, rows),
        )
        outputs = dict(
            penalty=jax.ShapeDtypeStruct((1, rows), f32),
            grad_w1=jax.ShapeDtypeStruct((piece, units), f32),
            grad_gain=jax.ShapeDtypeStruct((1, units), f32),
            grad_shift=jax.ShapeDtypeStruct((1, units), f32),
            grad_w2=jax.ShapeDtypeStruct((emb // nb, units), f32),
        )
        names = tuple(inputs) + tuple(outputs) + tuple(scratch)
        results = pl.pallas_call(
            make_kernel(ny, nz, npr, names, float(rows * nb)),
            out_shape=tuple(outputs.values()),
            in_specs=[whole] * len(inputs),
            out_specs=[here] * len(outputs),
            scratch_shapes=list(scratch.values()),
            compiler_params=pltpu.CompilerParams(
                collective_id=0, has_side_effects=True, vmem_limit_bytes=60 << 20
            ),
            name="head_step",
        )(*inputs.values())
        penalty, grad_w1, grad_gain, grad_shift, grad_w2 = pl.pallas_call(
            hand_over,
            out_shape=tuple(outputs.values()),
            in_specs=[whole] * len(outputs),
            out_specs=[whole] * len(outputs),
            scratch_shapes=[pltpu.SemaphoreType.DMA((len(outputs),))],
            name="hand_over",
        )(*results)
        return (
            penalty.reshape(rows),
            grad_w1,
            grad_gain.reshape(units),
            grad_shift.reshape(units),
            grad_w2.T,
        )

    return jax.shard_map(
        body,
        mesh=mesh,
        in_specs=(
            P("batch", None),
            P(None, "proto"),
            P("proto"),
            P("proto"),
            P("proto", None),
            P("proto", None),
            P("batch"),
        ),
        out_specs=(P("batch"), P("batch", "proto"), P("proto"), P("proto"), P("proto", "batch")),
        check_vma=False,
    )
```

```python
from types import SimpleNamespace

import jax
import jax.numpy as jnp
from jax import lax
from jax.experimental import pallas as pl
from jax.experimental.pallas import tpu as pltpu
from jax.sharding import PartitionSpec as P

ITERS = 3
MESH = pl.DeviceIdType.MESH
f32, bf16 = jnp.float32, jnp.bfloat16
CONTRACT_LAST = (((1,), (1,)), ((), ()))
CONTRACT_FIRST = (((0,), (0,)), ((), ()))

penalty_weighting = 64.0


def total(ref):
    count = ref.shape[0]
    chains = 4 if count >= 16 else 1
    sums = [ref[chain] for chain in range(chains)]
    for slot in range(chains, count):
        sums[slot % chains] = sums[slot % chains] + ref[slot]
    while len(sums) > 1:
        sums = [sums[i] + sums[i + 1] for i in range(0, len(sums), 2)]
    return sums[0]


def split(value):
    high = value.astype(bf16)
    low = (value - high.astype(f32)).astype(bf16)
    return jnp.concatenate([high, low], 0)


def make_kernel(ny, nz, npr, names, crops_all):
    def kernel(*refs):
        r = SimpleNamespace(**dict(zip(names, refs)))
        batch, proto = lax.axis_index("batch"), lax.axis_index("proto")
        y, z = batch // nz, batch % nz
        rings = {
            "y": (ny, y, lambda q: (q * nz + z, proto)),
            "z": (nz, z, lambda q: (y * nz + q, proto)),
            "p": (npr, proto, lambda q: (batch, q)),
        }
        send_sem, recv_sem, in_sem = r.send_sem, r.recv_sem, r.in_sem
        stages = []

        def send(source, target, stage, device):
            pltpu.make_async_remote_copy(
                src_ref=source,
                dst_ref=target,
                send_sem=send_sem.at[stage],
                recv_sem=recv_sem.at[stage],
                device_id=device,
                device_id_type=MESH,
            ).start()

        def new_stage(part):
            stages.append(part)
            return len(stages) - 1

        def exchange(axis, source_of, landing):
            count, me, device = rings[axis]
            stage = new_stage(landing.at[pl.ds(0, count - 1)])

            def step(offset, carry):
                peer = (me + offset) % count
                send(source_of(peer), landing.at[me], stage, device(peer))
                return carry

            lax.fori_loop(1, count, step, 0)
            landing[me] = source_of(me)[...]
            return stage

        def arrived(stage):
            pltpu.make_async_copy(stages[stage], stages[stage], recv_sem.at[stage]).wait()

        def sent(stage):
            pltpu.make_async_copy(stages[stage], stages[stage], send_sem.at[stage]).wait()

        def scatter(axis, source, landing, relay):
            count, me, device = rings[axis]
            far = count // 2
            stage_r, stage = new_stage(relay), new_stage(landing)
            turn = 1 - 2 * (proto % 2)

            def member(offset):
                return (me + turn * offset + count) % count

            send(source.at[member(far)], relay, stage_r, device(member(-1)))
            near = [o for d in range(far - 1, 0, -1) for o in (d, -d) if o != 1 - far]
            for slot, offset in enumerate(near):
                peer = member(offset)
                send(source.at[peer], landing.at[slot], stage, device(peer))

            def pass_on():
                arrived(stage_r)
                peer = member(1 - far)
                source[peer] = source[peer] + relay[...]
                send(source.at[peer], landing.at[len(near)], stage, device(peer))

            def result():
                arrived(stage)
                return total(landing) + source[me]

            return pass_on, result

        def sum_start(value, parts, landing):
            begun = []
            for h in range(2):
                parts[h] = value[:, h * 128 : (h + 1) * 128].reshape(parts.shape[1:])
                begun.append(exchange("p", lambda q: parts.at[h, q], landing.at[h]))
            return begun

        def sum_spread(begun, landing, own, everywhere):
            spread = []
            for h in range(2):
                arrived(begun[h])
                own[h] = total(landing.at[h])
                spread.append(exchange("p", lambda q: own.at[h], everywhere.at[h]))
            return spread

        def sum_end(spread, everywhere):
            sides = []
            for h in range(2):
                arrived(spread[h])
                side = everywhere[h]
                sides.append(side.reshape(side.shape[0] * side.shape[1], side.shape[2]))
            return jnp.concatenate(sides, 1)

        loads = [
            pltpu.make_async_copy(src, dst, in_sem.at[i])
            for i, (src, dst) in enumerate(
                (
                    (r.f_in, r.f),
                    (r.w1_in, r.w1),
                    (r.w2_in, r.w2),
                    (r.pr_in, r.pr),
                    (r.gain_in, r.gain),
                    (r.shift_in, r.shift),
                    (r.partner_in, r.partner),
                )
            )
        ]
        for load in loads:
            load.start()

        barrier = pltpu.get_barrier_semaphore()
        peers = 0
        for axis in ("y", "z", "p"):
            count, me, device = rings[axis]
            peers += count - 1

            def greet(offset, carry, count=count, me=me, device=device):
                pl.semaphore_signal(
                    barrier, inc=1, device_id=device((me + offset) % count), device_id_type=MESH
                )
                return carry

            lax.fori_loop(1, count, greet, 0)

        loads[0].wait()
        loads[1].wait()
        pre_act = jnp.dot(r.f[...], r.w1[...], preferred_element_type=f32)
        r.pre[...] = pre_act
        r.mom[0:1, :] = jnp.sum(pre_act, 0, keepdims=True)
        r.mom[1:2, :] = jnp.sum(pre_act * pre_act, 0, keepdims=True)
        pl.semaphore_wait(barrier, peers)
        stage = exchange("y", lambda q: r.mom, r.mom_y)
        r.fsum[...] = jnp.sum(r.f[...].astype(f32), 0, keepdims=True)
        stage_f = exchange("y", lambda q: r.fsum, r.fsum_y)
        rows, emb = r.f.shape[0], r.w2.shape[1]
        lanes = 128
        slab, piece = r.ft.shape[1], r.grad_w1.shape[0]
        features_t = r.f[...].astype(f32).T.astype(bf16).reshape(ny, slab, rows)
        r.ft[:, :, :rows] = features_t
        r.ft[:, :, rows:] = features_t
        arrived(stage)
        r.mom2[...] = total(r.mom_y)
        stage = exchange("z", lambda q: r.mom2, r.mom_z)

        def by_features(right, left_out, right_out):
            def step(i, carry):
                grad = jnp.dot(r.ft[i], right[...], preferred_element_type=f32)
                left_out[i] = grad[:, :lanes].reshape(nz, piece, lanes)
                for q in range(nz):
                    right_out[q, i] = grad[q * piece : (q + 1) * piece, lanes:]
                return carry

            lax.fori_loop(0, ny, step, 0)

        r.pair[0] = split(r.pre[...])
        by_features(r.pair.at[0], r.fna, r.fnb)
        pass_a, early_a = scatter("y", r.fna, r.fna_y, r.fna_r)
        pass_b, early_b = scatter("z", r.fnb, r.fnb_z, r.fnb_r)
        for load in loads[2:]:
            load.wait()
        arrived(stage)
        moments = total(r.mom_z)
        batch_mean = moments[0:1, :] / crops_all
        batch_var = moments[1:2, :] / crops_all - batch_mean * batch_mean
        inv_std = lax.rsqrt(batch_var + 1e-05)
        gain, shift = r.gain[...], r.shift[...]
        normed = (r.pre[...] - batch_mean) * inv_std
        shifted = gain * normed + shift
        hidden = jnp.maximum(shifted, 0.0).astype(bf16)
        r.normed[...] = normed
        r.shifted[...] = shifted
        r.hidden[...] = hidden

        part = jnp.dot(hidden, r.w2[...], preferred_element_type=f32)
        begun = sum_start(part, r.emb_part, r.emb_rs)
        chunks, width = r.u.shape[0], r.u.shape[1]

        def unit(j, carry):
            proto_float = r.pr[j].astype(f32)
            inv = lax.rsqrt(jnp.sum(proto_float * proto_float, 1, keepdims=True) + 1e-06)
            r.u[j] = (proto_float * inv).astype(bf16)
            return carry

        lax.fori_loop(0, chunks // 2, unit, 0)
        pass_a()
        pass_b()
        spread = sum_spread(begun, r.emb_rs, r.emb_own, r.emb_ag)
        lax.fori_loop(chunks // 2, chunks, unit, 0)
        arrived(stage_f)
        r.fsum2[...] = total(r.fsum_y)
        stage_f = exchange("z", lambda q: r.fsum2, r.fsum_z)
        raw_emb = sum_end(spread, r.emb_ag)
        inv_norm = lax.rsqrt(jnp.sum(raw_emb * raw_emb, 1, keepdims=True) + 1e-06)
        embedded = raw_emb * inv_norm
        emb_low = embedded.astype(bf16)
        r.embedded[...] = embedded
        r.emb_low[...] = emb_low
        r.inv_norm[...] = jnp.broadcast_to(inv_norm, r.inv_norm.shape)

        half = width // 2
        groups = width // lanes

        def columns(j, codes):
            mass = jnp.sum(codes, 0, keepdims=True)
            r.col_a[0, pl.ds(j, 1), :] = mass[:, :half]
            r.col_b[0, pl.ds(j, 1), :] = mass[:, half:]

        def score(j, acc):
            affinity = lax.dot_general(
                r.emb_low[...], r.u[j], CONTRACT_LAST, preferred_element_type=f32
            )
            raised = jnp.exp(affinity * 10.0)
            codes = raised * raised
            r.codes[j] = codes
            r.raised[j] = raised.astype(bf16)
            columns(j, codes)
            for g in range(groups):
                acc = acc + raised[:, g * lanes : (g + 1) * lanes]
            return acc

        denom_part = lax.fori_loop(0, chunks, score, jnp.zeros((rows, lanes), f32))

        def to_row(square):
            return jnp.sum(square.T, 0, keepdims=True)

        def to_columns(row):
            return jnp.broadcast_to(row, (rows, lanes)).T

        def row_sums(scale):
            def step(j, acc):
                codes = r.codes[j]
                weight_a = codes[:, :half] * r.scale_a[pl.ds(j, 1), :]
                weight_b = codes[:, half:] * r.scale_b[pl.ds(j, 1), :]
                for g in range(half // lanes):
                    acc = acc + weight_a[:, g * lanes : (g + 1) * lanes]
                    acc = acc + weight_b[:, g * lanes : (g + 1) * lanes]
                return acc

            return to_row(lax.fori_loop(0, chunks, step, jnp.zeros((rows, lanes), f32)))

        for it in range(ITERS):
            stage_a = exchange("y", lambda q: r.col_a.at[it], r.col_a1.at[it])
            stage_b = exchange("z", lambda q: r.col_b.at[it], r.col_b1.at[it])
            if it == 0:
                def soft(j, acc):
                    return acc + jnp.dot(r.raised[j], r.u[j], preferred_element_type=f32)

                soft_part = lax.fori_loop(0, chunks, soft, jnp.zeros((rows, emb), f32))
                begun = sum_start(soft_part, r.soft_part, r.soft_rs)
                r.row_src[0, 1:2, :] = to_row(denom_part)
            if it == 1:
                r.row_src[1, 1:2, :] = jnp.zeros((1, lanes), f32)
                r.fnas[...] = early_a()
                stage_na = exchange("z", lambda q: r.fnas.at[q], r.fna_z)
            if it == 2:
                arrived(stage_na)
                r.fn_own[:, :lanes] = total(r.fna_z)
                arrived(stage_nb)
                r.fn_own[:, lanes:] = total(r.fnb_y)
            arrived(stage_a)
            r.col_as[it] = total(r.col_a1.at[it])
            stage_a = exchange("z", lambda q: r.col_as.at[it], r.col_a2.at[it])
            arrived(stage_b)
            r.col_bs[it] = total(r.col_b1.at[it])
            stage_b = exchange("y", lambda q: r.col_bs.at[it], r.col_b2.at[it])
            if it == 1:
                r.fnbs[...] = early_b()
                stage_nb = exchange("y", lambda q: r.fnbs.at[q], r.fnb_y)
            arrived(stage_a)
            r.scale_a[...] = 1.0 / total(r.col_a2.at[it])
            arrived(stage_b)
            r.scale_b[...] = 1.0 / total(r.col_b2.at[it])
            if it == ITERS - 1:
                break
            r.row_src[it, 0:1, :] = row_sums(None)
            stage = exchange("p", lambda q: r.row_src.at[it], r.row_ag.at[it])
            if it == 0:
                soft_spread = sum_spread(begun, r.soft_rs, r.soft_own, r.soft_ag)
            if it == 1:
                arrived(stage_f)
                wanted = batch * piece + lax.broadcasted_iota(jnp.int32, (piece, ny * slab), 0)
                here = lax.broadcasted_iota(jnp.int32, (piece, ny * slab), 1) == wanted
                r.fsum_own[...] = jnp.broadcast_to(
                    jnp.sum(jnp.where(here, total(r.fsum_z), 0.0), 1, keepdims=True), (piece, lanes)
                )
            arrived(stage)
            masses = total(r.row_ag.at[it])
            if it == 0:
                r.denom[...] = masses[1:2, :]
            r.scale_rows[...] = to_columns(1.0 / masses[0:1, :])

            def column_sums(j, carry):
                scale = r.scale_rows[...]
                masses = [
                    jnp.sum(r.codes[j, :, g * lanes : (g + 1) * lanes] * scale, 0, keepdims=True)
                    for g in range(groups)
                ]
                r.col_a[it + 1, pl.ds(j, 1), :] = jnp.concatenate(masses[: groups // 2], 1)
                r.col_b[it + 1, pl.ds(j, 1), :] = jnp.concatenate(masses[groups // 2 :], 1)
                return carry

            lax.fori_loop(0, chunks, column_sums, 0)

        def target(j, carry):
            acc, grad = carry
            codes = r.codes[j]
            weight_a = codes[:, :half] * r.scale_a[pl.ds(j, 1), :]
            weight_b = codes[:, half:] * r.scale_b[pl.ds(j, 1), :]
            for g in range(half // lanes):
                acc = acc + weight_a[:, g * lanes : (g + 1) * lanes]
                acc = acc + weight_b[:, g * lanes : (g + 1) * lanes]
            grad = grad + jnp.dot(
                weight_a.astype(bf16), r.u[j, :half], preferred_element_type=f32
            )
            grad = grad + jnp.dot(
                weight_b.astype(bf16), r.u[j, half:], preferred_element_type=f32
            )
            return acc, grad

        row_part, target_part = lax.fori_loop(
            0, chunks, target, (jnp.zeros((rows, lanes), f32), jnp.zeros((rows, emb), f32))
        )
        begun = sum_start(target_part, r.tgt_part, r.tgt_rs)
        r.row_last[...] = to_row(row_part)
        stage_r = exchange("p", lambda q: r.row_last, r.row_last_ag)
        spread = sum_spread(begun, r.tgt_rs, r.tgt_own, r.tgt_ag)
        arrived(stage_r)
        scale_last = to_columns(1.0 / total(r.row_last_ag))
        denom = r.denom[...]
        denom_columns = to_columns(1.0 / denom)
        rows_iota = lax.broadcasted_iota(jnp.int32, (rows, rows), 0)
        swap = jnp.where(r.partner[...] == rows_iota, 1.0, 0.0).astype(f32)
        wide = lambda x: jnp.concatenate([x, x], 1)
        soft_grad = sum_end(soft_spread, r.soft_ag) * wide(denom_columns)
        own_target = sum_end(spread, r.tgt_ag) * wide(scale_last)
        partner_target = jnp.dot(
            swap, own_target, precision=lax.Precision.HIGHEST, preferred_element_type=f32
        )
        emb_grad = (soft_grad - partner_target) * (penalty_weighting * 10.0)
        embedded = r.embedded[...]
        inner = jnp.sum(embedded * emb_grad, 1, keepdims=True)
        raw_grad = ((emb_grad - embedded * inner) * r.inv_norm[:, 0:1]).astype(bf16)

        hidden_grad = lax.dot_general(
            raw_grad, r.w2[...], CONTRACT_LAST, preferred_element_type=f32
        )
        bn_grad = jnp.where(r.shifted[...] > 0, hidden_grad, 0.0)
        r.gsum[0:1, :] = jnp.sum(bn_grad, 0, keepdims=True)
        r.gsum[1:2, :] = jnp.sum(bn_grad * r.normed[...], 0, keepdims=True)
        stage = exchange("y", lambda q: r.gsum, r.gsum_y)
        r.pair[1] = split(bn_grad)
        by_features(r.pair.at[1], r.g1a, r.g1b)
        pass_a, late_a = scatter("y", r.g1a, r.g1a_y, r.g1a_r)
        pass_b, late_b = scatter("z", r.g1b, r.g1b_z, r.g1b_r)
        w2_grad = lax.dot_general(
            raw_grad, r.hidden[...], CONTRACT_FIRST, preferred_element_type=f32
        )
        r.g2a[...] = w2_grad[:, :lanes].reshape(ny, nz // 2, 8, lanes)
        right = w2_grad[:, lanes:].reshape(ny // 2, 2, nz // 2, 8, lanes)
        upper = lax.broadcasted_iota(jnp.int32, (nz // 2, 8, lanes), 1) < 4
        for i in range(ny // 2):
            one, two = right[i, 0], right[i, 1]
            r.g2b[:, 0, i] = jnp.where(upper, one, pltpu.roll(two, 4, 1))
            r.g2b[:, 1, i] = jnp.where(upper, pltpu.roll(one, 4, 1), two)
        stage_2a = exchange("y", lambda q: r.g2a.at[q], r.g2a_y)
        stage_2b = exchange("z", lambda q: r.g2b.at[q // 2, q % 2], r.g2b_z)
        score_dot = r.emb_low[...].astype(f32) * partner_target
        mismatch = to_row(score_dot[:, :lanes] + score_dot[:, lanes:])
        r.penalty[...] = jnp.log(denom) - mismatch * 10.0
        arrived(stage)
        r.gsum2[...] = total(r.gsum_y)
        stage = exchange("z", lambda q: r.gsum2, r.gsum_z)
        pass_a()
        pass_b()
        arrived(stage)
        sums = total(r.gsum_z)
        grad_shift, grad_gain = sums[0:1, :], sums[1:2, :]
        r.grad_shift[...] = grad_shift
        r.grad_gain[...] = grad_gain
        scale = gain * inv_std
        fsum = jnp.concatenate([r.fsum_own[...], r.fsum_own[...]], 1)
        by_normed = (r.fn_own[...] - fsum * batch_mean) * inv_std
        known = fsum * (grad_shift / crops_all) + by_normed * (grad_gain / crops_all)
        arrived(stage_2a)
        r.g2as[...] = total(r.g2a_y)
        stage_2a = exchange("z", lambda q: r.g2as.at[q // 2], r.g2a_z)
        arrived(stage_2b)
        r.g2bs[...] = total(r.g2b_z)
        stage_2b = exchange("y", lambda q: r.g2bs.at[q // 2], r.g2b_y)
        r.g1as[...] = late_a()
        stage_a = exchange("z", lambda q: r.g1as.at[q], r.g1a_z)
        r.g1bs[...] = late_b()
        stage_b = exchange("y", lambda q: r.g1bs.at[q], r.g1b_y)

        def own_half(tile, place):
            return jnp.where(place % 2 == 1, pltpu.roll(tile, 4, 0), tile)[0:4]

        arrived(stage_2a)
        r.grad_w2[:, :lanes] = own_half(total(r.g2a_z), z)
        arrived(stage_2b)
        r.grad_w2[:, lanes:] = own_half(total(r.g2b_y), y)
        arrived(stage_a)
        r.grad_w1[:, :lanes] = scale[:, :lanes] * (total(r.g1a_z) - known[:, :lanes])
        arrived(stage_b)
        r.grad_w1[:, lanes:] = scale[:, lanes:] * (total(r.g1b_y) - known[:, lanes:])
        for stage in range(len(stages)):
            sent(stage)

    return kernel


def hand_over(*refs):
    count = len(refs) // 2
    copies = [pltpu.make_async_copy(refs[i], refs[count + i], refs[-1].at[i]) for i in range(count)]
    for copy in copies:
        copy.start()
    for copy in copies:
        copy.wait()


def solution(mesh):
    nb, npr = mesh.shape["batch"], mesh.shape["proto"]
    ny = 1
    while (2 * ny) ** 2 <= nb:
        ny *= 2
    nz = nb // ny

    def body(features, w_first, bn_gain, bn_shift, w_second, prototypes, partner):
        rows, d_in = features.shape
        units, emb = w_second.shape
        protos = prototypes.shape[0]
        chunks = 8
        width = protos // chunks
        half = width // 2
        lanes = 128
        block = rows // npr
        slab, piece = d_in // ny, d_in // nb
        vmem = pltpu.VMEM
        scratch = dict(
            f=vmem((rows, d_in), bf16),
            w1=vmem((d_in, units), bf16),
            gain=vmem((1, units), f32),
            shift=vmem((1, units), f32),
            partner=vmem((1, rows), jnp.int32),
            w2=vmem((units, emb), bf16),
            pr=vmem((chunks, width, emb), bf16),
            u=vmem((chunks, width, emb), bf16),
            ft=vmem((ny, slab, 2 * rows), bf16),
            pair=vmem((2, 2 * rows, units), bf16),
            pre=vmem((rows, units), f32),
            mom=vmem((2, units), f32),
            mom_y=vmem((ny, 2, units), f32),
            mom2=vmem((2, units), f32),
            mom_z=vmem((nz, 2, units), f32),
            fsum=vmem((1, d_in), f32),
            fsum_y=vmem((ny, 1, d_in), f32),
            fsum2=vmem((1, d_in), f32),
            fsum_z=vmem((nz, 1, d_in), f32),
            fsum_own=vmem((piece, lanes), f32),
            fna=vmem((ny, nz, piece, lanes), f32),
            fnb=vmem((nz, ny, piece, lanes), f32),
            fna_y=vmem((ny - 2, nz, piece, lanes), f32),
            fnb_z=vmem((nz - 2, ny, piece, lanes), f32),
            fnas=vmem((nz, piece, lanes), f32),
            fnbs=vmem((ny, piece, lanes), f32),
            fna_z=vmem((nz, piece, lanes), f32),
            fnb_y=vmem((ny, piece, lanes), f32),
            fn_own=vmem((piece, units), f32),
            normed=vmem((rows, units), f32),
            shifted=vmem((rows, units), f32),
            hidden=vmem((rows, units), bf16),
            emb_part=vmem((2, npr, block, emb // 2), f32),
            emb_rs=vmem((2, npr, block, emb // 2), f32),
            emb_own=vmem((2, block, emb // 2), f32),
            emb_ag=vmem((2, npr, block, emb // 2), f32),
            embedded=vmem((rows, emb), f32),
            emb_low=vmem((rows, emb), bf16),
            inv_norm=vmem((rows, lanes), f32),
            codes=vmem((chunks, rows, width), f32),
            raised=vmem((chunks, rows, width), bf16),
            col_a=vmem((ITERS, chunks, half), f32),
            col_b=vmem((ITERS, chunks, half), f32),
            col_a1=vmem((ITERS, ny, chunks, half), f32),
            col_b1=vmem((ITERS, nz, chunks, half), f32),
            col_as=vmem((ITERS, chunks, half), f32),
            col_bs=vmem((ITERS, chunks, half), f32),
            col_a2=vmem((ITERS, nz, chunks, half), f32),
            col_b2=vmem((ITERS, ny, chunks, half), f32),
            scale_a=vmem((chunks, half), f32),
            scale_b=vmem((chunks, half), f32),
            soft_part=vmem((2, npr, block, emb // 2), f32),
            soft_rs=vmem((2, npr, block, emb // 2), f32),
            soft_own=vmem((2, block, emb // 2), f32),
            soft_ag=vmem((2, npr, block, emb // 2), f32),
            row_src=vmem((ITERS - 1, 2, rows), f32),
            row_ag=vmem((ITERS - 1, npr, 2, rows), f32),
            denom=vmem((1, rows), f32),
            scale_rows=vmem((rows, lanes), f32),
            tgt_part=vmem((2, npr, block, emb // 2), f32),
            tgt_rs=vmem((2, npr, block, emb // 2), f32),
            tgt_own=vmem((2, block, emb // 2), f32),
            tgt_ag=vmem((2, npr, block, emb // 2), f32),
            row_last=vmem((1, rows), f32),
            row_last_ag=vmem((npr, 1, rows), f32),
            gsum=vmem((2, units), f32),
            gsum_y=vmem((ny, 2, units), f32),
            gsum2=vmem((2, units), f32),
            gsum_z=vmem((nz, 2, units), f32),
            g2a=vmem((ny, nz // 2, 8, lanes), f32),
            g2b=vmem((nz // 2, 2, ny // 2, 8, lanes), f32),
            g2a_y=vmem((ny, nz // 2, 8, lanes), f32),
            g2b_z=vmem((nz, ny // 2, 8, lanes), f32),
            g2as=vmem((nz // 2, 8, lanes), f32),
            g2bs=vmem((ny // 2, 8, lanes), f32),
            g2a_z=vmem((nz, 8, lanes), f32),
            g2b_y=vmem((ny, 8, lanes), f32),
            g1a_r=vmem((nz, piece, lanes), f32),
            g1b_r=vmem((ny, piece, lanes), f32),
            fna_r=vmem((nz, piece, lanes), f32),
            fnb_r=vmem((ny, piece, lanes), f32),
            g1a=vmem((ny, nz, piece, lanes), f32),
            g1b=vmem((nz, ny, piece, lanes), f32),
            g1a_y=vmem((ny - 2, nz, piece, lanes), f32),
            g1b_z=vmem((nz - 2, ny, piece, lanes), f32),
            g1as=vmem((nz, piece, lanes), f32),
            g1bs=vmem((ny, piece, lanes), f32),
            g1a_z=vmem((nz, piece, lanes), f32),
            g1b_y=vmem((ny, piece, lanes), f32),
            send_sem=pltpu.SemaphoreType.DMA((64,)),
            recv_sem=pltpu.SemaphoreType.DMA((64,)),
            in_sem=pltpu.SemaphoreType.DMA((7,)),
        )
        whole = pl.BlockSpec(memory_space=pl.ANY)
        here = pl.BlockSpec(memory_space=pltpu.VMEM)
        inputs = dict(
            f_in=features,
            w1_in=w_first,
            gain_in=bn_gain.reshape(1, units),
            shift_in=bn_shift.reshape(1, units),
            w2_in=w_second,
            pr_in=prototypes.reshape(chunks, width, emb),
            partner_in=partner.reshape(1, rows),
        )
        outputs = dict(
            penalty=jax.ShapeDtypeStruct((1, rows), f32),
            grad_w1=jax.ShapeDtypeStruct((piece, units), f32),
            grad_gain=jax.ShapeDtypeStruct((1, units), f32),
            grad_shift=jax.ShapeDtypeStruct((1, units), f32),
            grad_w2=jax.ShapeDtypeStruct((emb // nb, units), f32),
        )
        names = tuple(inputs) + tuple(outputs) + tuple(scratch)
        results = pl.pallas_call(
            make_kernel(ny, nz, npr, names, float(rows * nb)),
            out_shape=tuple(outputs.values()),
            in_specs=[whole] * len(inputs),
            out_specs=[here] * len(outputs),
            scratch_shapes=list(scratch.values()),
            compiler_params=pltpu.CompilerParams(
                collective_id=0, has_side_effects=True, vmem_limit_bytes=60 << 20
            ),
            name="head_step",
        )(*inputs.values())
        penalty, grad_w1, grad_gain, grad_shift, grad_w2 = pl.pallas_call(
            hand_over,
            out_shape=tuple(outputs.values()),
            in_specs=[whole] * len(outputs),
            out_specs=[whole] * len(outputs),
            scratch_shapes=[pltpu.SemaphoreType.DMA((len(outputs),))],
            name="hand_over",
        )(*results)
        return (
            penalty.reshape(rows),
            grad_w1,
            grad_gain.reshape(units),
            grad_shift.reshape(units),
            grad_w2.T,
        )

    return jax.shard_map(
        body,
        mesh=mesh,
        in_specs=(
            P("batch", None),
            P(None, "proto"),
            P("proto"),
            P("proto"),
            P("proto", None),
            P("proto", None),
            P("batch"),
        ),
        out_specs=(P("batch"), P("batch", "proto"), P("proto"), P("proto"), P("proto", "batch")),
        check_vma=False,
    )
```
